32 devices in a mesh: row: 8 (over z, y), col: 4 (over x, core).
Axes of the slice: x: 2, y: 2, z: 4, core: 2. Of those that a mesh axis runs over, the one named last changes fastest.
Arguments:
- anc_inverse: float32 [20480, 20480], P('row', 'col'), may hold values from -6 to 6
- l_store: float32 [4, 20480, 256], P('col', 'row'), may hold values from -0.0546875 to 0.0546875
- diag_inv: float32 [4, 256, 256], P('col'), may hold values from -6 to 6
- block_lists: int32 [4, 96], replicated, may hold values from 0 to 159, as said below
- block_counts: int32 [4], replicated, may hold values from 48 to 96, as said below
- sibling_columns: int32 [4], replicated, may hold values from 0 to 3, as said below
Outputs:
- upper_out: float32 [4, 256, 20480], P(None, 'row', 'col')
- lower_out: float32 [4, 20480, 256], P('col', 'row')
- diag_out: float32 [4, 256, 256], P('col')
The draws below stay inside these ranges and needn't reach their ends.
Inputs may be any that keep to these rules, and one draw needn't show every extreme that they name: `block_lists`: in each sibling's row the entries are distinct block indices; entries at positions from block_counts onward are ignored. `block_counts`: some sibling uses all 96 entries. `sibling_columns`: distinct columns for distinct siblings.
All inputs are finite; a program needn't handle non-finite values.
Results may differ from the reference program's by a relative error of at most 0.00011.
Values sent between devices are 32-bit elements; how exact they have to be, the bound alone decides.
A program may use at most 128 MiB of HBM per device.

```python
import jax
import jax.numpy as jnp
from jax import lax

BLK = 128
NBLK = 160
W = 256
SIB = 4
KMAX = 96
S = 20480
N_COL = 4


def draw_block_lists(key, part):
    sib_keys = jax.random.split(jax.random.fold_in(key, 3), SIB)
    picked = jax.vmap(lambda one_key: jax.random.permutation(one_key, NBLK)[:KMAX])(sib_keys)
    return picked.astype(jnp.int32)


def draw_block_counts(key, part):
    counts = jax.random.randint(jax.random.fold_in(key, 7), (SIB,), KMAX // 2, KMAX + 1)
    pick_one = jax.random.randint(jax.random.fold_in(key, 8), (), 0, SIB)
    counts = jnp.where(jnp.arange(SIB) == pick_one, KMAX, counts)
    return counts.astype(jnp.int32)


def draw_sibling_columns(key, part):
    column_order = jax.random.permutation(jax.random.fold_in(key, 11), N_COL)
    return column_order[:SIB].astype(jnp.int32)


def block_levels(key, dims, cuts, smallest, high):
    def one(axis_at, parts):
        draws = jax.random.uniform(jax.random.fold_in(jax.random.fold_in(key, 6), axis_at), (parts,), jnp.float32, smallest / len(cuts), high / len(cuts))
        return jnp.repeat(jnp.exp(draws), dims[axis_at] // parts).reshape((-1,) + (1,) * (len(dims) - axis_at - 1))

    level = one(*cuts[0])
    for cut in cuts[1:]:
        level = level * one(*cut)
    return level


def gaussian(own_key, extent, scale, limit, cuts=(), kind=jnp.bfloat16):
    result = scale * jax.random.normal(own_key, extent, jnp.float32)
    if cuts:
        result = result * block_levels(own_key, extent, cuts, -0.22, 0.18)
    return jnp.clip(result, -limit, limit).astype(kind)


def setup_inputs(seed: int = 0) -> dict:
    streams_of = jax.random.split(jax.random.key(seed), 7)
    anc_inverse = gaussian(streams_of[0], (S, S), 1.0, 6.0, ((0, 8), (1, 4)), jnp.float32)
    l_store = gaussian(streams_of[1], (N_COL, S, W), (KMAX * BLK) ** -0.5, 0.0546875, ((0, 4), (1, 8)), jnp.float32)
    diag_inv = gaussian(streams_of[2], (N_COL, W, W), 1.0, 6.0, ((0, 4),), jnp.float32)
    block_lists = draw_block_lists(jax.random.fold_in(streams_of[6], 71), 0)
    block_counts = draw_block_counts(jax.random.fold_in(streams_of[6], 71), 0)
    sibling_columns = draw_sibling_columns(jax.random.fold_in(streams_of[6], 71), 0)
    return dict(anc_inverse=anc_inverse, l_store=l_store, diag_inv=diag_inv, block_lists=block_lists, block_counts=block_counts, sibling_columns=sibling_columns)


def member_mask(block_lists, block_counts):
    block_ids = jnp.arange(NBLK, dtype=jnp.int32)
    valid_entry = jnp.arange(KMAX, dtype=jnp.int32)[None, :] < block_counts[:, None]
    entry_hits = (block_lists[:, :, None] == block_ids[None, None, :]) & valid_entry[:, :, None]
    return jnp.repeat(jnp.any(entry_hits, axis=1).astype(jnp.float32), BLK, axis=1)


def reference(anc_inverse, l_store, diag_inv, block_lists, block_counts, sibling_columns):
    listed = member_mask(block_lists, block_counts)
    panels = l_store[sibling_columns.astype(jnp.int32)] * listed[:, :, None]
    upper_out = -jnp.einsum("jsw,st->jwt", panels, anc_inverse, precision=lax.Precision.HIGHEST, preferred_element_type=jnp.float32) * listed[:, None, :]
    inner_sum = jnp.einsum("jws,jsv->jwv", upper_out, panels, precision=lax.Precision.HIGHEST, preferred_element_type=jnp.float32)
    chosen = (sibling_columns[:, None] == jnp.arange(N_COL, dtype=jnp.int32)[None, :]).astype(jnp.float32)
    present = jnp.sum(chosen, axis=0)
    lower_out = jnp.einsum("jc,jws->csw", chosen, upper_out, precision=lax.Precision.HIGHEST, preferred_element_type=jnp.float32)
    diag_out = present[:, None, None] * diag_inv - jnp.einsum("jc,jwv->cwv", chosen, inner_sum, precision=lax.Precision.HIGHEST, preferred_element_type=jnp.float32)
    return upper_out, lower_out, diag_out
```

```python
import functools

import jax
import jax.numpy as jnp
from jax import lax
from jax.experimental import pallas as pl
from jax.experimental.pallas import tpu as pltpu
from jax.sharding import PartitionSpec as P

BLK = 128
MESH = pl.DeviceIdType.MESH


def listed_table(block_lists, block_counts, block_total):
    block_ids = jnp.arange(block_total, dtype=jnp.int32)
    valid_entry = jnp.arange(block_lists.shape[1], dtype=jnp.int32)[None, :] < block_counts[:, None]
    entry_hits = (block_lists[:, :, None] == block_ids[None, None, :]) & valid_entry[:, :, None]
    return jnp.any(entry_hits, axis=1)


def product_kernel(siblings, tile_blocks, col_blocks, row_blocks,
                   slot_ref, rows_ref, count_ref, column_ref,
                   a_ref, panels_ref, out_ref, a_high, a_low, p_high, p_low, acc):
    stripe = pl.program_id(0)
    width = out_ref.shape[0]

    @pl.when(stripe == 0)
    def _():
        for sibling in range(siblings):
            column = column_ref[sibling]

            @pl.loop(0, row_blocks)
            def _(block):
                lanes = pl.ds(pl.multiple_of(block * BLK, BLK), BLK)
                value = panels_ref[pl.ds(pl.multiple_of(column * width, width), width), lanes]
                high = value.astype(jnp.bfloat16)
                p_high[sibling, block] = high
                p_low[sibling, block] = (value - high.astype(jnp.float32)).astype(jnp.bfloat16)

            p_high[sibling, row_blocks] = jnp.zeros(p_high.shape[2:], jnp.bfloat16)
            p_low[sibling, row_blocks] = jnp.zeros(p_low.shape[2:], jnp.bfloat16)

    @pl.loop(0, row_blocks)
    def _(block):
        rows = pl.ds(pl.multiple_of(block * BLK, BLK), BLK)
        value = a_ref[rows, :]
        high = value.astype(jnp.bfloat16)
        a_high[block] = high
        a_low[block] = (value - high.astype(jnp.float32)).astype(jnp.bfloat16)

    for sibling in range(siblings):
        acc[...] = jnp.zeros_like(acc)
        base = sibling * (row_blocks + 1)

        @pl.loop(0, (count_ref[sibling] + 1) // 2)
        def _(pair):
            first = rows_ref[base + 2 * pair]
            second = rows_ref[base + 2 * pair + 1]
            second_a = jnp.minimum(second, row_blocks - 1)
            ph = [p_high[sibling, first], p_high[sibling, second]]
            plo = [p_low[sibling, first], p_low[sibling, second]]
            ah = [a_high[first], a_high[second_a]]
            al = [a_low[first], a_low[second_a]]
            left = jnp.concatenate(ph + ph + plo, axis=1)
            right = jnp.concatenate(ah + al + ah, axis=0)
            acc[...] += jnp.dot(left, right, preferred_element_type=jnp.float32)

        for block in range(tile_blocks):
            slot = slot_ref[sibling * col_blocks + stripe * tile_blocks + block]

            @pl.when(slot >= 0)
            def _():
                out_ref[:, pl.ds(pl.multiple_of(slot * BLK, BLK), BLK)] = (
                    -acc[:, block * BLK:(block + 1) * BLK]
                )


def product(slot, rows, counts, columns, anc, panels, width, cap):
    siblings = counts.shape[0]
    depth, cells = anc.shape
    row_blocks, col_blocks = depth // BLK, cells // BLK
    tile_blocks = next(n for n in (4, 2, 1) if col_blocks % n == 0)
    tile = tile_blocks * BLK
    return pl.pallas_call(
        functools.partial(product_kernel, siblings, tile_blocks, col_blocks, row_blocks),
        out_shape=jax.ShapeDtypeStruct((width, cap * BLK), jnp.float32),
        grid_spec=pltpu.PrefetchScalarGridSpec(
            num_scalar_prefetch=4,
            grid=(col_blocks // tile_blocks,),
            in_specs=[
                pl.BlockSpec((depth, tile), lambda i, *_: (0, i)),
                pl.BlockSpec(panels.shape, lambda i, *_: (0, 0), pipeline_mode=pl.Buffered(1)),
            ],
            out_specs=pl.BlockSpec((width, cap * BLK), lambda i, *_: (0, 0), pipeline_mode=pl.Buffered(1)),
            scratch_shapes=[
                pltpu.VMEM((row_blocks, BLK, tile), jnp.bfloat16),
                pltpu.VMEM((row_blocks, BLK, tile), jnp.bfloat16),
                pltpu.VMEM((siblings, row_blocks + 1, width, BLK), jnp.bfloat16),
                pltpu.VMEM((siblings, row_blocks + 1, width, BLK), jnp.bfloat16),
                pltpu.VMEM((width, tile), jnp.float32),
            ],
        ),
        compiler_params=pltpu.CompilerParams(
            dimension_semantics=("arbitrary",), vmem_limit_bytes=63 * 1024 * 1000
        ),
    )(slot, rows, counts, columns, anc, panels)


def flip_kernel(value_ref, out_ref):
    out_ref[...] = value_ref[...].T


def flipped(value):
    depth, width = value.shape
    step = next(n for n in (512, 256, 128) if depth % n == 0)
    return pl.pallas_call(
        flip_kernel,
        out_shape=jax.ShapeDtypeStruct((width, depth), value.dtype),
        grid=(depth // step,),
        in_specs=[pl.BlockSpec((step, width), lambda i: (i, 0))],
        out_specs=pl.BlockSpec((width, step), lambda i: (0, i)),
    )(value)


def expand_kernel(siblings, col_count, col_blocks, slot_ref, owner_ref, compact_ref, upper_ref, slots_ref):
    @pl.loop(0, col_blocks)
    def _(block):
        lanes = pl.ds(pl.multiple_of(block * BLK, BLK), BLK)
        for sibling in range(siblings):
            slot = slot_ref[sibling * col_blocks + block]
            at = pl.ds(pl.multiple_of(jnp.maximum(slot, 0) * BLK, BLK), BLK)
            value = compact_ref[:, at]
            upper_ref[sibling, :, lanes] = jnp.where(slot >= 0, value, jnp.zeros_like(value))

    for column in range(col_count):
        sibling = owner_ref[column]
        value = upper_ref[jnp.maximum(sibling, 0)]
        slots_ref[column] = jnp.where(sibling >= 0, value, jnp.zeros_like(value))


def expand(slot, owner, compact, siblings, col_blocks):
    col_count = owner.shape[0]
    rows = compact.shape[0]
    return pl.pallas_call(
        functools.partial(expand_kernel, siblings, col_count, col_blocks),
        out_shape=(
            jax.ShapeDtypeStruct((siblings, rows, col_blocks * BLK), jnp.float32),
            jax.ShapeDtypeStruct((col_count, rows, col_blocks * BLK), jnp.float32),
        ),
        in_specs=[pl.BlockSpec(memory_space=pltpu.SMEM)] * 2 + [pl.BlockSpec(memory_space=pltpu.VMEM)],
        out_specs=(pl.BlockSpec(memory_space=pltpu.VMEM),) * 2,
    )(slot, owner, compact)


def finish_kernel(row_count, col_count,
                  slots_ref, own_ref, base_ref, lower_ref, diag_ref,
                  picked, inner, part, reduced, total,
                  send_sem, recv_sem, part_send, part_recv, total_send, total_recv):
    r, c = lax.axis_index("row"), lax.axis_index("col")
    ratio = row_count // col_count
    source_col = r // ratio
    slice_rows, cells = picked.shape[1], picked.shape[2]
    on_path = source_col == c

    barrier = pltpu.get_barrier_semaphore()
    for k in range(ratio):
        for target in range(col_count):
            @pl.when((c * ratio + k != r) | (c != target))
            def _():
                pl.semaphore_signal(barrier, inc=1, device_id=(c * ratio + k, target), device_id_type=MESH)
    for peer in range(row_count):
        @pl.when((peer != r) | (source_col != c))
        def _():
            pl.semaphore_signal(barrier, inc=1, device_id=(peer, source_col), device_id_type=MESH)

        @pl.when(peer != r)
        def _():
            pl.semaphore_signal(barrier, inc=1, device_id=(peer, c), device_id_type=MESH)
    expected = ratio * col_count + row_count + row_count - 1
    pl.semaphore_wait(barrier, expected - 2 * on_path.astype(jnp.int32))

    def block_copy(k, target):
        index = k * col_count + target
        return pltpu.make_async_remote_copy(
            src_ref=slots_ref.at[target, :, pl.ds(k * cells, cells)],
            dst_ref=picked.at[r],
            send_sem=send_sem.at[index],
            recv_sem=recv_sem.at[r],
            device_id=(c * ratio + k, target),
            device_id_type=MESH,
        )

    def local_copy(k, target):
        return pltpu.make_async_copy(
            slots_ref.at[target, :, pl.ds(k * cells, cells)], picked.at[r], recv_sem.at[r]
        )

    for k in range(ratio):
        for target in range(col_count):
            here = (c * ratio + k == r) & (c == target)

            @pl.when(here)
            def _():
                local_copy(k, target).start()

            @pl.when(jnp.logical_not(here))
            def _():
                block_copy(k, target).start()

    def arrived(source):
        return pltpu.make_async_remote_copy(
            src_ref=slots_ref.at[0, :, pl.ds(0, cells)],
            dst_ref=picked.at[source],
            send_sem=send_sem.at[0],
            recv_sem=recv_sem.at[source],
            device_id=(source, source_col),
            device_id_type=MESH,
        )

    for k in range(ratio):
        for target in range(col_count):
            here = (c * ratio + k == r) & (c == target)

            @pl.when(here)
            def _():
                local_copy(k, target).wait()
    for source in range(row_count):
        @pl.when((source != r) | (source_col != c))
        def _():
            arrived(source).wait_recv()

    step = 256 if cells % 256 == 0 else BLK
    inner[...] = jnp.zeros_like(inner)

    @pl.loop(0, cells // step)
    def _(i):
        at = pl.ds(pl.multiple_of(i * step, step), step)
        block = picked[:, :, at].reshape(row_count * slice_rows, step)
        inner[...] += jnp.dot(
            block, own_ref[at, :], precision=lax.Precision.HIGHEST, preferred_element_type=jnp.float32
        )

    def part_copy(peer):
        return pltpu.make_async_remote_copy(
            src_ref=inner.at[pl.ds(peer * slice_rows, slice_rows), :],
            dst_ref=part.at[r],
            send_sem=part_send.at[peer],
            recv_sem=part_recv.at[r],
            device_id=(peer, c),
            device_id_type=MESH,
        )

    def part_arrived(peer):
        return pltpu.make_async_remote_copy(
            src_ref=inner.at[pl.ds(0, slice_rows), :],
            dst_ref=part.at[peer],
            send_sem=part_send.at[peer],
            recv_sem=part_recv.at[peer],
            device_id=(peer, c),
            device_id_type=MESH,
        )

    def total_copy(peer):
        return pltpu.make_async_remote_copy(
            src_ref=reduced,
            dst_ref=total.at[r],
            send_sem=total_send.at[peer],
            recv_sem=total_recv.at[r],
            device_id=(peer, c),
            device_id_type=MESH,
        )

    def total_arrived(peer):
        return pltpu.make_async_remote_copy(
            src_ref=reduced,
            dst_ref=total.at[peer],
            send_sem=total_send.at[peer],
            recv_sem=total_recv.at[peer],
            device_id=(peer, c),
            device_id_type=MESH,
        )

    def peers(action):
        for peer in range(row_count):
            @pl.when(peer != r)
            def _():
                action(peer)

    peers(lambda peer: part_copy(peer).start())
    peers(lambda peer: part_arrived(peer).wait_recv())
    mine = inner[pl.ds(pl.multiple_of(r * slice_rows, slice_rows), slice_rows), :]
    for peer in range(row_count):
        @pl.when(peer == r)
        def _():
            part[peer] = mine
    value = part[0]
    for peer in range(1, row_count):
        value = value + part[peer]
    reduced[...] = value
    peers(lambda peer: total_copy(peer).start())

    @pl.loop(0, cells // step)
    def _(i):
        at = pl.ds(pl.multiple_of(i * step, step), step)
        block = picked[:, :, at].reshape(row_count * slice_rows, step)
        lower_ref[at, :] = block.T

    peers(lambda peer: total_arrived(peer).wait_recv())
    for peer in range(row_count):
        @pl.when(peer == r)
        def _():
            total[peer] = reduced[...]
    diag_ref[...] = base_ref[...] - total[...].reshape(diag_ref.shape)

    for k in range(ratio):
        for target in range(col_count):
            @pl.when((c * ratio + k != r) | (c != target))
            def _():
                block_copy(k, target).wait_send()
    peers(lambda peer: part_copy(peer).wait_send())
    peers(lambda peer: total_copy(peer).wait_send())


def finish(slots, own, base, row_count):
    col_count, slice_rows, _ = slots.shape
    cells, width = own.shape
    ratio = row_count // col_count
    vmem = pl.BlockSpec(memory_space=pltpu.VMEM)
    dma = pltpu.SemaphoreType.DMA
    return pl.pallas_call(
        functools.partial(finish_kernel, row_count, col_count),
        out_shape=(
            jax.ShapeDtypeStruct((cells, width), jnp.float32),
            jax.ShapeDtypeStruct((width, width), jnp.float32),
        ),
        in_specs=[vmem] * 3,
        out_specs=(vmem, vmem),
        scratch_shapes=[
            pltpu.VMEM((row_count, slice_rows, cells), jnp.float32),
            pltpu.VMEM((width, width), jnp.float32),
            pltpu.VMEM((row_count, slice_rows, width), jnp.float32),
            pltpu.VMEM((slice_rows, width), jnp.float32),
            pltpu.VMEM((row_count, slice_rows, width), jnp.float32),
            dma((ratio * col_count,)),
            dma((row_count,)),
            dma((row_count,)),
            dma((row_count,)),
            dma((row_count,)),
            dma((row_count,)),
        ],
        compiler_params=pltpu.CompilerParams(collective_id=0, has_side_effects=True),
    )(slots, own, base)


def per_device(anc_inverse, l_store, diag_inv, block_lists, block_counts, sibling_columns):
    siblings = block_lists.shape[0]
    row_count, col_count = lax.axis_size("row"), lax.axis_size("col")
    r, c = lax.axis_index("row"), lax.axis_index("col")
    row_blocks, col_blocks = anc_inverse.shape[0] // BLK, anc_inverse.shape[1] // BLK
    panels = lax.all_gather(flipped(l_store[0]), "col", tiled=True)

    table = listed_table(block_lists, block_counts, row_blocks * row_count)
    row_listed = lax.dynamic_slice_in_dim(table, r * row_blocks, row_blocks, axis=1)
    col_listed = lax.dynamic_slice_in_dim(table, c * col_blocks, col_blocks, axis=1)
    row_ints = row_listed.astype(jnp.int32)
    counts = jnp.sum(row_ints, axis=1)
    place = jnp.cumsum(row_ints, axis=1) - 1
    ids = jnp.arange(row_blocks, dtype=jnp.int32)
    entry = jnp.arange(row_blocks + 1, dtype=jnp.int32)
    hits = row_listed[:, :, None] & (place[:, :, None] == entry[None, None, :])
    rows = jnp.sum(jnp.where(hits, ids[None, :, None], 0), axis=1)
    rows = jnp.where(entry[None, :] < counts[:, None], rows, row_blocks).astype(jnp.int32).reshape(-1)

    flat = col_listed.reshape(-1)
    slot = jnp.where(flat, jnp.cumsum(flat.astype(jnp.int32)) - 1, -1).astype(jnp.int32)
    per_column = jnp.sum(table.reshape(siblings, col_count, col_blocks).astype(jnp.int32), axis=(0, 2))
    needed = jnp.max(per_column)
    slots_all = siblings * col_blocks
    caps = sorted({-(-slots_all * n // 40) for n in (19, 21, 23, 25, 28, 32, 40)})
    level = jnp.sum((needed > jnp.array(caps[:-1], jnp.int32)).astype(jnp.int32))

    match = sibling_columns[:, None] == jnp.arange(col_count, dtype=jnp.int32)[None, :]
    owner = jnp.max(
        jnp.where(match, jnp.arange(siblings, dtype=jnp.int32)[:, None], -1), axis=0
    ).astype(jnp.int32)
    mine = sibling_columns == c
    own_listed = jnp.any(row_listed & mine[:, None], axis=0)
    own = l_store[0] * jnp.repeat(own_listed.astype(jnp.float32), BLK)[:, None]
    base = jnp.sum(mine.astype(jnp.float32)) * diag_inv[0]

    def branch(cap):
        def run(anc, panels):
            partial_value = product(slot, rows, counts, sibling_columns, anc, panels, l_store.shape[2], cap)
            compact = lax.psum_scatter(partial_value, "row", scatter_dimension=0, tiled=True)
            return expand(slot, owner, compact, siblings, col_blocks)
        return run

    upper, slots = lax.switch(level, [branch(cap) for cap in caps], anc_inverse, panels)
    lower, diag = finish(slots, own, base, row_count)
    return upper, lower[None], diag[None]


def solution(mesh):
    return jax.shard_map(
        per_device,
        mesh=mesh,
        in_specs=(P("row", "col"), P("col", "row", None), P("col", None, None), P(), P(), P()),
        out_specs=(P(None, "row", "col"), P("col", "row", None), P("col", None, None)),
        check_vma=False,
    )
```
